32 devices in a mesh: row: 4 (over y, core), col: 8 (over z, x).
Axes of the slice: x: 2, y: 2, z: 4, core: 2. Of those that a mesh axis runs over, the one named last changes fastest.
Arguments:
- kernel: float32 [4, 4, 256, 2, 8, 256], P(None, 'row', None, None, 'col'), may hold values from -40 to 40, as said below
Outputs:
- trailing: float32 [4, 4, 256, 2, 8, 256], P(None, 'row', None, None, 'col')
- panels: float32 [4, 4, 256, 3, 256], P(None, 'row')
The draws below stay inside these ranges and needn't reach their ends.
Inputs may be any that keep to these rules, and one draw needn't show every extreme that they name: kernel is symmetric and positive definite with smallest eigenvalue at least 1.
All inputs are finite; a program needn't handle non-finite values.
Results may differ from the reference program's by a relative error of at most 0.0003.
Values sent between devices are 32-bit elements; how exact they have to be, the bound alone decides.
A program may use at most 128 MiB of HBM per device.

```python
import jax
import jax.numpy as jnp
from jax import lax

TILE = 256
FEATURES = 1024
STEPS = 3
COL_TILES = 2
TILES = 16
ROW_TILES = 4
ORDER = 4096


def draw_kernel(key, part):
    key_main = jax.random.fold_in(key, 11)
    features = jax.random.normal(key_main, (ORDER, FEATURES), jnp.float32)
    gram = jnp.dot(features, features.T, precision=lax.Precision.HIGHEST) / FEATURES
    gram = gram + jnp.eye(ORDER, dtype=jnp.float32)
    return gram.reshape(ROW_TILES, TILES // ROW_TILES, TILE, COL_TILES, TILES // COL_TILES, TILE)


def setup_inputs(seed: int = 0) -> dict:
    streams_of = jax.random.split(jax.random.key(seed), 2)
    kernel = draw_kernel(jax.random.fold_in(streams_of[1], 71), 0)
    return dict(kernel=kernel)


def reference(kernel):
    shape_in = kernel.shape
    order = shape_in[0] * shape_in[1] * shape_in[2]
    tile_size = shape_in[2]
    working = kernel.reshape(order, order)
    identity = jnp.eye(tile_size, dtype=jnp.float32)
    row_ids = jnp.arange(order)
    collected = []
    for panel_step in range(STEPS):
        start = panel_step * tile_size
        finish = start + tile_size
        factor = jnp.linalg.cholesky(working[start:finish, start:finish])
        inverse = lax.linalg.triangular_solve(factor, identity, left_side=True, lower=True)
        panel = jnp.dot(working[:, start:finish], inverse.T, precision=lax.Precision.HIGHEST)
        panel = jnp.where((row_ids >= start)[:, None], panel, jnp.float32(0.0))
        collected.append(panel)
        lower = panel[finish:]
        updated = working[finish:, finish:] - jnp.dot(lower, lower.T, precision=lax.Precision.HIGHEST)
        working = jnp.zeros((order, order), jnp.float32).at[finish:, finish:].set(updated)
    trailing = working.reshape(shape_in)
    panels = jnp.stack(collected, axis=1).reshape(shape_in[0], shape_in[1], tile_size, STEPS, tile_size)
    return (trailing, panels)
```

```python
import functools

import jax
import jax.numpy as jnp
from jax import lax
from jax.experimental import pallas as pl
from jax.experimental.pallas import tpu as pltpu
from jax.sharding import PartitionSpec as P

STEPS = 3
PANEL = 16
MESH = pl.DeviceIdType.MESH
F32 = jnp.float32
BF16 = jnp.bfloat16
LOWER = [(i, j) for j in range(STEPS) for i in range(j, STEPS)]
SLOT = {ij: n for n, ij in enumerate(LOWER)}


def split_col(cols):
    width = 1
    while width * width * 4 <= cols:
        width *= 2
    return width, cols // width


def exchange_kernel(R, C, x_ref, ld_ref, rs_ref, cs_ref, send_sem, local_sem, ld_sem, ldx_sem, rs_sem, cs_sem):
    A, B, T, _ = x_ref.shape
    X, Z = split_col(C)
    r, c = lax.axis_index("row"), lax.axis_index("col")
    z, x = lax.div(c, X), lax.rem(c, X)
    chunk = T // R
    pending = []
    counts = {"send": 0, "local": 0}

    def send(cond, src, dst, sem, dev):
        n = counts["send"]
        counts["send"] += 1
        copy = pltpu.make_async_remote_copy(
            src_ref=src, dst_ref=dst, send_sem=send_sem.at[n], recv_sem=sem, device_id=dev, device_id_type=MESH
        )
        pl.when(cond)(copy.start)
        pending.append((cond, copy.wait_send))

    def local(cond, src, dst):
        n = counts["local"]
        counts["local"] += 1
        copy = pltpu.make_async_copy(src, dst, local_sem.at[n])
        pl.when(cond)(copy.start)
        return copy.wait

    def wait_recv(cond, dst, sem):
        copy = pltpu.make_async_remote_copy(
            src_ref=dst, dst_ref=dst, send_sem=send_sem.at[0], recv_sem=sem,
            device_id=(lax.rem(r + 1, R), c), device_id_type=MESH,
        )
        pl.when(cond)(copy.wait_recv)

    def rows_of(n, q):
        return ld_ref.at[n, pl.ds(pl.multiple_of(q * chunk, chunk), chunk), :]

    def part(ref, q):
        return ref.at[pl.ds(pl.multiple_of(q * chunk, chunk), chunk), :]

    ld_local = []
    for n, (i, j) in enumerate(LOWER):
        src = x_ref.at[i // R, j // C]
        owner = (r == i % R) & (c == j % C)
        for step in range(1, R):
            q = lax.rem(r + step, R)
            send(owner, part(src, q), rows_of(n, q), ld_sem.at[n], (q, c))
        ld_local.append(local(owner, part(src, r), rows_of(n, r)))
    rs_local = {}
    for k in range(STEPS):
        for a in range(A):
            rs_local[k, a] = local(c == k % C, x_ref.at[a, k // C], rs_ref.at[k, a])
    cs_local = {}
    for k in range(STEPS):
        for b in range(B):
            src, dst = x_ref.at[k // R, b], cs_ref.at[k, b]
            for step in range(1, R):
                send(r == k % R, src, dst, cs_sem.at[k, b], (lax.rem(r + step, R), c))
            cs_local[k, b] = local(r == k % R, src, dst)

    def spread(slot, sem, source, lane):
        zs, xs = divmod(source, X)
        if lane != xs:
            send(c == source, slot, slot, sem, (r, zs * X + lane))
        on = x == lane
        send(on & (z >= zs) & (z + 1 < Z), slot, slot, sem, (r, lax.rem(c + X, C)))
        send(on & (z <= zs) & (z > 0), slot, slot, sem, (r, lax.rem(c + C - X, C)))
        for other in range(X):
            if other != lane:
                cond = on & (z != zs) if other == xs else on
                send(cond, slot, slot, sem, (r, z * X + other))

    for n, (i, j) in enumerate(LOWER):
        owner = (r == i % R) & (c == j % C)
        slot = rows_of(n, r)
        pl.when(owner)(ld_local[n])
        wait_recv(jnp.logical_not(owner), slot, ld_sem.at[n])
        spread(slot, ld_sem.at[n], j % C, n % X)
        for step in range(1, R):
            q = lax.rem(r + step, R)
            send(r >= 0, slot, slot, ldx_sem.at[n, step - 1], (q, c))
    for a in range(A):
        for k in range(STEPS):
            slot = rs_ref.at[k, a]
            pl.when(c == k % C)(rs_local[k, a])
            wait_recv(c != k % C, slot, rs_sem.at[k, a])
            spread(slot, rs_sem.at[k, a], k % C, k % X if k < X else a % X)
    for n in range(len(LOWER)):
        for step in range(1, R):
            q = lax.rem(r + R - step, R)
            wait_recv(r >= 0, rows_of(n, q), ldx_sem.at[n, step - 1])
    for k in range(STEPS):
        for b in range(B):
            pl.when(r == k % R)(cs_local[k, b])
            wait_recv(r != k % R, cs_ref.at[k, b], cs_sem.at[k, b])
    for cond, wait in pending:
        pl.when(cond)(wait)


def exchange(tiles, R, C):
    A, B, T, _ = tiles.shape
    X, _ = split_col(C)
    n = len(LOWER)
    vmem = pl.BlockSpec(memory_space=pltpu.VMEM)
    sends = n * (R - 1) * 2 + STEPS * B * (R - 1) + (n + STEPS * A) * (X + 2)
    locals_ = n + STEPS * A + STEPS * B
    dma = pltpu.SemaphoreType.DMA
    return pl.pallas_call(
        functools.partial(exchange_kernel, R, C),
        name="exchange",
        out_shape=(
            jax.ShapeDtypeStruct((n, T, T), F32),
            jax.ShapeDtypeStruct((STEPS, A, T, T), F32),
            jax.ShapeDtypeStruct((STEPS, B, T, T), F32),
        ),
        in_specs=[vmem],
        out_specs=(vmem, vmem, vmem),
        scratch_shapes=[dma((sends,)), dma((locals_,)), dma((n,)), dma((n, R - 1)), dma((STEPS, A)), dma((STEPS, B))],
        compiler_params=pltpu.CompilerParams(has_side_effects=True, vmem_limit_bytes=56 * 2**20),
    )(tiles)


def dot_nt(p, q):
    return lax.dot_general(p, q, (((1,), (1,)), ((), ())), precision=lax.Precision.HIGHEST, preferred_element_type=F32)


def dot_nn(p, q):
    return lax.dot_general(p, q, (((1,), (0,)), ((), ())), precision=lax.Precision.HIGHEST, preferred_element_type=F32)


def invert_factor(w_ref):
    T = w_ref.shape[0]
    b = PANEL
    lane = lax.broadcasted_iota(jnp.int32, (b, T), 1)
    sub = lax.broadcasted_iota(jnp.int32, (b, T), 0)
    row = lax.broadcasted_iota(jnp.int32, (T, T), 0)
    col = lax.broadcasted_iota(jnp.int32, (T, T), 1)

    def body(p, carry):
        base = pl.multiple_of(p * b, b)
        R = w_ref[pl.ds(base, b), :]
        E = jnp.where(lane == base + sub, F32(1.0), F32(0.0))
        cols = []
        for j in range(b):
            picked = jnp.sum(jnp.where(lane == base + j, R, F32(0.0)), axis=1, keepdims=True)
            cols.append(jnp.broadcast_to(picked, (b, T)))
        diag = jnp.ones((b, T), F32)
        for j in range(b):
            d = jnp.broadcast_to(cols[j][j : j + 1, :], (b, T))
            diag = jnp.where(sub == j, d, diag)
            if j == b - 1:
                break
            w = jnp.where(sub > j, cols[j] * (F32(1.0) / d), F32(0.0))
            for i in range(j + 1, b):
                cols[i] = cols[i] - w * cols[i][j : j + 1, :]
            R = R - w * R[j : j + 1, :]
            E = E - w * E[j : j + 1, :]
        scale = lax.rsqrt(diag)
        R = R * scale
        E = E * scale
        V = jnp.where((lane >= base) & (lane < base + b), E, R)
        coef = jnp.where(lane >= base + b, R, F32(0.0))
        update = lax.dot_general(
            coef, V, (((0,), (0,)), ((), ())), precision=lax.Precision.HIGHEST, preferred_element_type=F32
        )
        drop = (row >= base + b) & (col >= base) & (col < base + b)
        w_ref[...] = jnp.where(drop, F32(0.0), w_ref[...]) - update
        w_ref[pl.ds(base, b), :] = V
        return carry

    lax.fori_loop(0, T // b, body, 0)
    w_ref[...] = jnp.where(row >= col, w_ref[...], F32(0.0))


def factor_kernel(ld_ref, m_ref, w_ref):
    for n in range(len(LOWER)):
        w_ref[n] = ld_ref[n]
    for k in range(STEPS):
        invert_factor(w_ref.at[SLOT[k, k]])
        inv = w_ref[SLOT[k, k]]
        for i in range(k + 1, STEPS):
            w_ref[SLOT[i, k]] = dot_nt(w_ref[SLOT[i, k]], inv)
        for j in range(k + 1, STEPS):
            for i in range(j, STEPS):
                w_ref[SLOT[i, j]] = w_ref[SLOT[i, j]] - dot_nt(w_ref[SLOT[i, k]], w_ref[SLOT[j, k]])
    for k in range(STEPS):
        m_ref[SLOT[k, k]] = w_ref[SLOT[k, k]]
        for i in range(k + 1, STEPS):
            total = dot_nn(w_ref[SLOT[i, k]], m_ref[SLOT[k, k]])
            for j in range(k + 1, i):
                total = total + dot_nn(w_ref[SLOT[i, j]], m_ref[SLOT[j, k]])
            m_ref[SLOT[i, k]] = -dot_nn(w_ref[SLOT[i, i]], total)


def factor(lead):
    vmem = pl.BlockSpec(memory_space=pltpu.VMEM)
    return pl.pallas_call(
        factor_kernel,
        name="factor",
        out_shape=jax.ShapeDtypeStruct(lead.shape, F32),
        in_specs=[vmem],
        out_specs=vmem,
        scratch_shapes=[pltpu.VMEM(lead.shape, F32)],
        compiler_params=pltpu.CompilerParams(vmem_limit_bytes=56 * 2**20),
    )(lead)


def halves(value):
    high = value.astype(BF16)
    return high, (value - high.astype(F32)).astype(BF16)


def dot3(p, q, dims):
    d = functools.partial(lax.dot_general, dimension_numbers=(dims, ((), ())), preferred_element_type=F32)
    return d(p[0], q[0]) + (d(p[0], q[1]) + d(p[1], q[0]))


NT = ((1,), (1,))
NN = ((1,), (0,))


def finish_kernel(R, C, x_ref, m_ref, rs_ref, cs_ref, t_ref, p_ref, mh_ref, ml_ref, qh_ref, ql_ref):
    A, B, T, _ = x_ref.shape
    r, c = lax.axis_index("row"), lax.axis_index("col")
    for n in range(len(LOWER)):
        mh_ref[n], ml_ref[n] = halves(m_ref[n])
    for b in range(B):
        terms = [halves(cs_ref[j, b]) for j in range(STEPS)]
        for k in range(STEPS):
            total = None
            for j in range(k + 1):
                n = SLOT[k, j]
                term = dot3((mh_ref[n], ml_ref[n]), terms[j], NN)
                total = term if total is None else total + term
            qh_ref[k, b], ql_ref[k, b] = halves(total)

    def body(a, carry):
        tile_row = a * R + r
        terms = [halves(rs_ref[j, a]) for j in range(STEPS)]
        panel = []
        for k in range(STEPS):
            total = None
            for j in range(k + 1):
                n = SLOT[k, j]
                term = dot3(terms[j], (mh_ref[n], ml_ref[n]), NT)
                total = term if total is None else total + term
            p_ref[a, k] = jnp.where(tile_row >= k, total, F32(0.0))
            panel.append(halves(total))
        for b in range(B):
            total = x_ref[a, b]
            for k in range(STEPS):
                total = total - dot3(panel[k], (qh_ref[k, b], ql_ref[k, b]), NN)
            keep = (tile_row >= STEPS) & (b * C + c >= STEPS)
            t_ref[a, :, b * T : (b + 1) * T] = jnp.where(keep, total, F32(0.0))
        return carry

    lax.fori_loop(0, A, body, 0)


def finish(tiles, m, rs, cs, R, C):
    A, B, T, _ = tiles.shape
    vmem = pl.BlockSpec(memory_space=pltpu.VMEM)
    n = len(LOWER)
    return pl.pallas_call(
        functools.partial(finish_kernel, R, C),
        name="finish",
        out_shape=(jax.ShapeDtypeStruct((A, T, B * T), F32), jax.ShapeDtypeStruct((A, STEPS, T, T), F32)),
        in_specs=[vmem] * 4,
        out_specs=(vmem, vmem),
        scratch_shapes=[
            pltpu.VMEM((n, T, T), BF16),
            pltpu.VMEM((n, T, T), BF16),
            pltpu.VMEM((STEPS, B, T, T), BF16),
            pltpu.VMEM((STEPS, B, T, T), BF16),
        ],
        compiler_params=pltpu.CompilerParams(vmem_limit_bytes=56 * 2**20),
    )(tiles, m, rs, cs)


def shards(kernel):
    A, _, T, B, _, _ = kernel.shape
    R, C = lax.axis_size("row"), lax.axis_size("col")
    tiles = kernel.reshape(A, T, B, T).transpose(0, 2, 1, 3)
    ld, rs, cs = exchange(tiles, R, C)
    m = factor(ld)
    trailing, panels = finish(tiles, m, rs, cs, R, C)
    return trailing.reshape(kernel.shape), panels.transpose(0, 2, 1, 3).reshape(A, 1, T, STEPS, T)


def solution(mesh):
    in_specs = (P(None, "row", None, None, "col", None),)
    out_specs = (P(None, "row", None, None, "col", None), P(None, "row", None, None, None))
    return jax.shard_map(shards, mesh=mesh, in_specs=in_specs, out_specs=out_specs, check_vma=False)
```

```python
import functools

import jax
import jax.numpy as jnp
from jax import lax
from jax.experimental import pallas as pl
from jax.experimental.pallas import tpu as pltpu
from jax.sharding import PartitionSpec as P

STEPS = 3
PANEL = 16
GROUPS = 4
SKEW = 2
MESH = pl.DeviceIdType.MESH
F32 = jnp.float32
BF16 = jnp.bfloat16
LOWER = [(i, j) for j in range(STEPS) for i in range(j, STEPS)]
SLOT = {ij: n for n, ij in enumerate(LOWER)}


def split_col(cols):
    width = 1
    while width * width * 4 <= cols:
        width *= 2
    return width, cols // width


def dot_nt(p, q):
    return lax.dot_general(p, q, (((1,), (1,)), ((), ())), precision=lax.Precision.HIGHEST, preferred_element_type=F32)


def dot_nn(p, q):
    return lax.dot_general(p, q, (((1,), (0,)), ((), ())), precision=lax.Precision.HIGHEST, preferred_element_type=F32)


def invert_factor(w_ref, between):
    T = w_ref.shape[0]
    b = PANEL
    lane = lax.broadcasted_iota(jnp.int32, (b, T), 1)
    sub = lax.broadcasted_iota(jnp.int32, (b, T), 0)
    row = lax.broadcasted_iota(jnp.int32, (T, T), 0)
    col = lax.broadcasted_iota(jnp.int32, (T, T), 1)

    def body(p, carry):
        base = pl.multiple_of(p * b, b)
        R = w_ref[pl.ds(base, b), :]
        E = jnp.where(lane == base + sub, F32(1.0), F32(0.0))
        cols = []
        for j in range(b):
            picked = jnp.sum(jnp.where(lane == base + j, R, F32(0.0)), axis=1, keepdims=True)
            cols.append(jnp.broadcast_to(picked, (b, T)))
        diag = jnp.ones((b, T), F32)
        for j in range(b):
            d = jnp.broadcast_to(cols[j][j : j + 1, :], (b, T))
            diag = jnp.where(sub == j, d, diag)
            if j == b - 1:
                break
            w = jnp.where(sub > j, cols[j] * (F32(1.0) / d), F32(0.0))
            for i in range(j + 1, b):
                cols[i] = cols[i] - w * cols[i][j : j + 1, :]
            R = R - w * R[j : j + 1, :]
            E = E - w * E[j : j + 1, :]
        scale = lax.rsqrt(diag)
        R = R * scale
        E = E * scale
        V = jnp.where((lane >= base) & (lane < base + b), E, R)
        coef = jnp.where(lane >= base + b, R, F32(0.0))
        update = lax.dot_general(
            coef, V, (((0,), (0,)), ((), ())), precision=lax.Precision.HIGHEST, preferred_element_type=F32
        )
        drop = (row >= base + b) & (col >= base) & (col < base + b)
        w_ref[...] = jnp.where(drop, F32(0.0), w_ref[...]) - update
        w_ref[pl.ds(base, b), :] = V
        return carry

    inner = T // b // GROUPS

    def group(g, carry):
        lax.fori_loop(g * inner, (g + 1) * inner, body, 0)
        between(g)
        return carry

    lax.fori_loop(0, GROUPS, group, 0)
    w_ref[...] = jnp.where(row >= col, w_ref[...], F32(0.0))


def lead_kernel(
    R, C, x_ref, m_ref, rs_ref, cs_ref, ld_ref, w_ref,
    send_sem, local_sem, ld_sem, ldx_sem, rs_sem, cs_sem, rs_send, rs_loc,
):
    A, B, T, _ = x_ref.shape
    X, Z = split_col(C)
    r, c = lax.axis_index("row"), lax.axis_index("col")
    z, x = lax.div(c, X), lax.rem(c, X)
    chunk = T // R
    items = A * STEPS
    pending = []
    counts = {"send": 0, "local": 0}

    def send(cond, src, dst, sem, dev):
        n = counts["send"]
        counts["send"] += 1
        copy = pltpu.make_async_remote_copy(
            src_ref=src, dst_ref=dst, send_sem=send_sem.at[n], recv_sem=sem, device_id=dev, device_id_type=MESH
        )
        pl.when(cond)(copy.start)
        pending.append((cond, copy.wait_send))

    def local(cond, src, dst):
        n = counts["local"]
        counts["local"] += 1
        copy = pltpu.make_async_copy(src, dst, local_sem.at[n])
        pl.when(cond)(copy.start)
        return copy.wait

    def wait_recv(cond, dst, sem):
        copy = pltpu.make_async_remote_copy(
            src_ref=dst, dst_ref=dst, send_sem=send_sem.at[0], recv_sem=sem,
            device_id=(lax.rem(r + 1, R), c), device_id_type=MESH,
        )
        pl.when(cond)(copy.wait_recv)

    def part(ref, q):
        return ref.at[pl.ds(pl.multiple_of(q * chunk, chunk), chunk), :]

    ld_local = []
    for n, (i, j) in enumerate(LOWER):
        src = x_ref.at[i // R, j // C]
        owner = (r == i % R) & (c == j % C)
        for step in range(1, R):
            q = lax.rem(r + step, R)
            send(owner, part(src, q), part(ld_ref.at[n], q), ld_sem.at[n], (q, c))
        ld_local.append(local(owner, part(src, r), part(ld_ref.at[n], r)))

    def item(m):
        k, a = lax.rem(m, STEPS), lax.div(m, STEPS)
        source = lax.rem(k, C)
        zs, xs = lax.div(source, X), lax.rem(source, X)
        lane = jnp.where(k < X, lax.rem(k, X), lax.rem(a, X))
        return k, a, source, zs, xs, lane

    def own_copy(m):
        k, a, source, _, _, _ = item(m)
        copy = pltpu.make_async_copy(x_ref.at[a, lax.div(k, C)], rs_ref.at[k, a], rs_loc.at[m])
        return c == source, copy

    def spread(m):
        k, a, source, zs, xs, lane = item(m)
        on = x == lane
        slot = rs_ref.at[k, a]

        def copy(n, dev):
            return pltpu.make_async_remote_copy(
                src_ref=slot, dst_ref=slot, send_sem=rs_send.at[m, n], recv_sem=rs_sem.at[m],
                device_id=dev, device_id_type=MESH,
            )

        yield (c == source) & (xs != lane), copy(0, (r, lax.rem(zs * X + lane, C)))
        yield on & (z >= zs) & (z + 1 < Z), copy(1, (r, lax.rem(c + X, C)))
        yield on & (z <= zs) & (z > 0), copy(2, (r, lax.rem(c + C - X, C)))
        for step in range(1, X):
            other = lax.rem(lane + step, X)
            yield on & jnp.logical_not((z == zs) & (other == xs)), copy(2 + step, (r, z * X + other))

    def start_own(m, carry):
        cond, copy = own_copy(m)
        pl.when(cond)(copy.start)
        return carry

    lax.fori_loop(0, items, start_own, 0)

    def lead_step(n, when):
        i, j = LOWER[n]
        owner = (r == i % R) & (c == j % C)
        slot = part(ld_ref.at[n], r)
        pl.when(owner & when)(ld_local[n])
        wait_recv(jnp.logical_not(owner) & when, slot, ld_sem.at[n])
        return slot

    def lead_swap(n, slot, when):
        for step in range(1, R):
            send(when, slot, slot, ldx_sem.at[n, step - 1], (lax.rem(r + step, R), c))

    for early in (True, False):
        for n, (i, j) in enumerate(LOWER):
            lane, source = n % X, j % C
            zs, xs = divmod(source, X)
            on = x == lane
            first = on | (c == source)
            when = first if early else jnp.logical_not(first)
            slot = lead_step(n, when)
            if early:
                if lane != xs:
                    send(c == source, slot, slot, ld_sem.at[n], (r, zs * X + lane))
                send(on & (z >= zs) & (z + 1 < Z), slot, slot, ld_sem.at[n], (r, lax.rem(c + X, C)))
                send(on & (z <= zs) & (z > 0), slot, slot, ld_sem.at[n], (r, lax.rem(c + C - X, C)))
                for other in range(X):
                    if other != lane:
                        cond = on & (z != zs) if other == xs else on
                        send(cond, slot, slot, ld_sem.at[n], (r, z * X + other))
            lead_swap(n, slot, when)

    def own_spread(m, carry):
        cond, copy = own_copy(m)
        pl.when(cond)(copy.wait)
        for go, out in spread(m):
            pl.when(cond & go)(out.start)
        return carry

    lax.fori_loop(0, items, own_spread, 0)

    cs_local = {}
    for k in range(STEPS):
        for b in range(B):
            src, dst = x_ref.at[k // R, b], cs_ref.at[k, b]
            for step in range(1, R):
                send(r == k % R, src, dst, cs_sem.at[k, b], (lax.rem(r + step, R), c))
            cs_local[k, b] = local(r == k % R, src, dst)

    def take(m):
        k, a, _, _, _, _ = item(m)
        return pltpu.make_async_remote_copy(
            src_ref=rs_ref.at[k, a], dst_ref=rs_ref.at[k, a], send_sem=send_sem.at[0], recv_sem=rs_sem.at[m],
            device_id=(lax.rem(r + 1, R), c), device_id_type=MESH,
        )

    skew = SKEW * jnp.maximum(z - 1, 0)
    deepest = SKEW * max(Z - 2, 0)
    per_slot = -(-items // (STEPS * GROUPS))

    def forward(s):
        m = s - skew

        @pl.when((m >= 0) & (m < items))
        def _():
            _, _, source, _, _, lane = item(m)

            @pl.when((x == lane) & (c != source))
            def _():
                take(m).wait_recv()
                for go, out in spread(m):
                    pl.when(go)(out.start)

    def slot_work(s):
        for u in range(per_slot):
            forward(s * per_slot + u)

    def lead_tile(n):
        for step in range(1, R):
            q = lax.rem(r + R - step, R)
            wait_recv(r >= 0, part(ld_ref.at[n], q), ldx_sem.at[n, step - 1])
        w_ref[n] = ld_ref[n]

    lead_tile(0)
    for k in range(STEPS):
        invert_factor(w_ref.at[SLOT[k, k]], lambda g, k=k: slot_work(k * GROUPS + g))
        inv = w_ref[SLOT[k, k]]
        if k == 0:
            for n in range(1, len(LOWER)):
                lead_tile(n)
        for i in range(k + 1, STEPS):
            w_ref[SLOT[i, k]] = dot_nt(w_ref[SLOT[i, k]], inv)
        for j in range(k + 1, STEPS):
            for i in range(j, STEPS):
                w_ref[SLOT[i, j]] = w_ref[SLOT[i, j]] - dot_nt(w_ref[SLOT[i, k]], w_ref[SLOT[j, k]])
    for k in range(STEPS):
        m_ref[SLOT[k, k]] = w_ref[SLOT[k, k]]
        for i in range(k + 1, STEPS):
            total = dot_nn(w_ref[SLOT[i, k]], m_ref[SLOT[k, k]])
            for j in range(k + 1, i):
                total = total + dot_nn(w_ref[SLOT[i, j]], m_ref[SLOT[j, k]])
            m_ref[SLOT[i, k]] = -dot_nn(w_ref[SLOT[i, i]], total)

    def late(s, carry):
        forward(s)
        return carry

    lax.fori_loop(STEPS * GROUPS * per_slot, max(items + deepest, STEPS * GROUPS * per_slot), late, 0)

    def finish_item(m, carry):
        _, _, source, _, _, lane = item(m)
        pl.when((x != lane) & (c != source))(take(m).wait_recv)
        for go, out in spread(m):
            pl.when(go)(out.wait_send)
        return carry

    lax.fori_loop(0, items, finish_item, 0)
    for k in range(STEPS):
        for b in range(B):
            pl.when(r == k % R)(cs_local[k, b])
            wait_recv(r != k % R, cs_ref.at[k, b], cs_sem.at[k, b])
    for cond, wait in pending:
        pl.when(cond)(wait)


def lead(tiles, R, C):
    A, B, T, _ = tiles.shape
    X, _ = split_col(C)
    n = len(LOWER)
    items = STEPS * A
    vmem = pl.BlockSpec(memory_space=pltpu.VMEM)
    sends = n * (R - 1) * 3 + STEPS * B * (R - 1) + n * (X + 2)
    locals_ = n + STEPS * B
    dma = pltpu.SemaphoreType.DMA
    return pl.pallas_call(
        functools.partial(lead_kernel, R, C),
        name="lead",
        out_shape=(
            jax.ShapeDtypeStruct((n, T, T), F32),
            jax.ShapeDtypeStruct((STEPS, A, T, T), F32),
            jax.ShapeDtypeStruct((STEPS, B, T, T), F32),
        ),
        in_specs=[vmem],
        out_specs=(vmem, vmem, vmem),
        scratch_shapes=[
            pltpu.VMEM((n, T, T), F32),
            pltpu.VMEM((n, T, T), F32),
            dma((sends,)), dma((locals_,)), dma((n,)), dma((n, R - 1)), dma((items,)), dma((STEPS, B)),
            dma((items, X + 2)), dma((items,)),
        ],
        compiler_params=pltpu.CompilerParams(has_side_effects=True, vmem_limit_bytes=56 * 2**20),
    )(tiles)


def halves(value):
    high = value.astype(BF16)
    return high, (value - high.astype(F32)).astype(BF16)


def dot3(p, q, dims):
    d = functools.partial(lax.dot_general, dimension_numbers=(dims, ((), ())), preferred_element_type=F32)
    return d(p[0], q[0]) + (d(p[0], q[1]) + d(p[1], q[0]))


NT = ((1,), (1,))
NN = ((1,), (0,))


def finish_kernel(R, C, x_ref, m_ref, rs_ref, cs_ref, t_ref, p_ref, mh_ref, ml_ref, qh_ref, ql_ref):
    A, B, T, _ = x_ref.shape
    r, c = lax.axis_index("row"), lax.axis_index("col")
    for n in range(len(LOWER)):
        mh_ref[n], ml_ref[n] = halves(m_ref[n])
    for b in range(B):
        terms = [halves(cs_ref[j, b]) for j in range(STEPS)]
        for k in range(STEPS):
            total = None
            for j in range(k + 1):
                n = SLOT[k, j]
                term = dot3((mh_ref[n], ml_ref[n]), terms[j], NN)
                total = term if total is None else total + term
            qh_ref[k, b], ql_ref[k, b] = halves(total)

    def body(a, carry):
        tile_row = a * R + r
        terms = [halves(rs_ref[j, a]) for j in range(STEPS)]
        panel = []
        for k in range(STEPS):
            total = None
            for j in range(k + 1):
                n = SLOT[k, j]
                term = dot3(terms[j], (mh_ref[n], ml_ref[n]), NT)
                total = term if total is None else total + term
            p_ref[a, k] = jnp.where(tile_row >= k, total, F32(0.0))
            panel.append(halves(total))
        for b in range(B):
            total = x_ref[a, b]
            for k in range(STEPS):
                total = total - dot3(panel[k], (qh_ref[k, b], ql_ref[k, b]), NN)
            keep = (tile_row >= STEPS) & (b * C + c >= STEPS)
            t_ref[a, :, b * T : (b + 1) * T] = jnp.where(keep, total, F32(0.0))
        return carry

    lax.fori_loop(0, A, body, 0)


def finish(tiles, m, rs, cs, R, C):
    A, B, T, _ = tiles.shape
    vmem = pl.BlockSpec(memory_space=pltpu.VMEM)
    n = len(LOWER)
    return pl.pallas_call(
        functools.partial(finish_kernel, R, C),
        name="finish",
        out_shape=(jax.ShapeDtypeStruct((A, T, B * T), F32), jax.ShapeDtypeStruct((A, STEPS, T, T), F32)),
        in_specs=[vmem] * 4,
        out_specs=(vmem, vmem),
        scratch_shapes=[
            pltpu.VMEM((n, T, T), BF16),
            pltpu.VMEM((n, T, T), BF16),
            pltpu.VMEM((STEPS, B, T, T), BF16),
            pltpu.VMEM((STEPS, B, T, T), BF16),
        ],
        compiler_params=pltpu.CompilerParams(vmem_limit_bytes=56 * 2**20),
    )(tiles, m, rs, cs)


def shards(kernel):
    A, _, T, B, _, _ = kernel.shape
    R, C = lax.axis_size("row"), lax.axis_size("col")
    tiles = kernel.reshape(A, T, B, T).transpose(0, 2, 1, 3)
    m, rs, cs = lead(tiles, R, C)
    trailing, panels = finish(tiles, m, rs, cs, R, C)
    return trailing.reshape(kernel.shape), panels.transpose(0, 2, 1, 3).reshape(A, 1, T, STEPS, T)


def solution(mesh):
    in_specs = (P(None, "row", None, None, "col", None),)
    out_specs = (P(None, "row", None, None, "col", None), P(None, "row", None, None, None))
    return jax.shard_map(shards, mesh=mesh, in_specs=in_specs, out_specs=out_specs, check_vma=False)
```

```python
import functools

import jax
import jax.numpy as jnp
from jax import lax
from jax.experimental import pallas as pl
from jax.experimental.pallas import tpu as pltpu
from jax.sharding import PartitionSpec as P

STEPS = 3
PANEL = 16
GROUPS = 8
SKEW = 0
PIECES = 2
MESH = pl.DeviceIdType.MESH
F32 = jnp.float32
BF16 = jnp.bfloat16
LOWER = [(i, j) for j in range(STEPS) for i in range(j, STEPS)]
SLOT = {ij: n for n, ij in enumerate(LOWER)}


def split_col(cols):
    width = 1
    while width * width * 4 <= cols:
        width *= 2
    return width, cols // width


def dot_nt(p, q):
    return lax.dot_general(p, q, (((1,), (1,)), ((), ())), precision=lax.Precision.HIGHEST, preferred_element_type=F32)


def dot_nn(p, q):
    return lax.dot_general(p, q, (((1,), (0,)), ((), ())), precision=lax.Precision.HIGHEST, preferred_element_type=F32)


def invert_factor(w_ref, between):
    T = w_ref.shape[0]
    b = PANEL
    lane = lax.broadcasted_iota(jnp.int32, (b, T), 1)
    sub = lax.broadcasted_iota(jnp.int32, (b, T), 0)
    row = lax.broadcasted_iota(jnp.int32, (T, T), 0)
    col = lax.broadcasted_iota(jnp.int32, (T, T), 1)

    def body(p, carry):
        base = pl.multiple_of(p * b, b)
        R = w_ref[pl.ds(base, b), :]
        E = jnp.where(lane == base + sub, F32(1.0), F32(0.0))
        cols = []
        for j in range(b):
            picked = jnp.sum(jnp.where(lane == base + j, R, F32(0.0)), axis=1, keepdims=True)
            cols.append(jnp.broadcast_to(picked, (b, T)))
        diag = jnp.ones((b, T), F32)
        for j in range(b):
            d = jnp.broadcast_to(cols[j][j : j + 1, :], (b, T))
            diag = jnp.where(sub == j, d, diag)
            if j == b - 1:
                break
            w = jnp.where(sub > j, cols[j] * (F32(1.0) / d), F32(0.0))
            for i in range(j + 1, b):
                cols[i] = cols[i] - w * cols[i][j : j + 1, :]
            R = R - w * R[j : j + 1, :]
            E = E - w * E[j : j + 1, :]
        scale = lax.rsqrt(diag)
        R = R * scale
        E = E * scale
        V = jnp.where((lane >= base) & (lane < base + b), E, R)
        coef = jnp.where(lane >= base + b, R, F32(0.0))
        update = lax.dot_general(
            coef, V, (((0,), (0,)), ((), ())), precision=lax.Precision.HIGHEST, preferred_element_type=F32
        )
        drop = (row >= base + b) & (col >= base) & (col < base + b)
        w_ref[...] = jnp.where(drop, F32(0.0), w_ref[...]) - update
        w_ref[pl.ds(base, b), :] = V
        return carry

    inner = T // b // GROUPS

    def group(g, carry):
        lax.fori_loop(g * inner, (g + 1) * inner, body, 0)
        between(g)
        return carry

    lax.fori_loop(0, GROUPS, group, 0)
    w_ref[...] = jnp.where(row >= col, w_ref[...], F32(0.0))


def lead_kernel(
    R, C, x_ref, m_ref, rs_ref, cs_ref, ld_ref, w_ref,
    send_sem, local_sem, ld_sem, ldx_sem, rs_sem, cs_sem, rs_send, rs_loc,
):
    A, B, T, _ = x_ref.shape
    X, Z = split_col(C)
    r, c = lax.axis_index("row"), lax.axis_index("col")
    z, x = lax.div(c, X), lax.rem(c, X)
    chunk = T // R
    items = A * STEPS * PIECES
    pending = []
    counts = {"send": 0, "local": 0}

    def send(cond, src, dst, sem, dev):
        n = counts["send"]
        counts["send"] += 1
        copy = pltpu.make_async_remote_copy(
            src_ref=src, dst_ref=dst, send_sem=send_sem.at[n], recv_sem=sem, device_id=dev, device_id_type=MESH
        )
        pl.when(cond)(copy.start)
        pending.append((cond, copy.wait_send))

    def local(cond, src, dst):
        n = counts["local"]
        counts["local"] += 1
        copy = pltpu.make_async_copy(src, dst, local_sem.at[n])
        pl.when(cond)(copy.start)
        return copy.wait

    def wait_recv(cond, dst, sem):
        copy = pltpu.make_async_remote_copy(
            src_ref=dst, dst_ref=dst, send_sem=send_sem.at[0], recv_sem=sem,
            device_id=(lax.rem(r + 1, R), c), device_id_type=MESH,
        )
        pl.when(cond)(copy.wait_recv)

    def part(ref, q):
        return ref.at[pl.ds(pl.multiple_of(q * chunk, chunk), chunk), :]

    ld_local = []
    for n, (i, j) in enumerate(LOWER):
        src = x_ref.at[i // R, j // C]
        owner = (r == i % R) & (c == j % C)
        for step in range(1, R):
            q = lax.rem(r + step, R)
            send(owner, part(src, q), part(ld_ref.at[n], q), ld_sem.at[n], (q, c))
        ld_local.append(local(owner, part(src, r), part(ld_ref.at[n], r)))

    def item(m):
        tile, piece = lax.div(m, PIECES), lax.rem(m, PIECES)
        rest = jnp.maximum(tile - A, 0)
        k = jnp.where(tile < A, STEPS - 1, lax.rem(rest, STEPS - 1))
        a = jnp.where(tile < A, tile, lax.div(rest, STEPS - 1))
        source = lax.rem(k, C)
        zs, xs = lax.div(source, X), lax.rem(source, X)
        lane = jnp.where(k < X, lax.rem(k, X), lax.rem(a, X))
        return k, a, piece, source, zs, xs, lane

    def need(m):
        return item(m)[1] * R + r >= STEPS

    def piece_of(m):
        k, a, piece = item(m)[:3]
        rows = T // PIECES
        return rs_ref.at[k, a, pl.ds(pl.multiple_of(piece * rows, rows), rows), :]

    def own_copy(m):
        k, a, piece, source = item(m)[:4]
        rows = T // PIECES
        src = x_ref.at[a, lax.div(k, C), pl.ds(pl.multiple_of(piece * rows, rows), rows), :]
        return (c == source) & need(m), pltpu.make_async_copy(src, piece_of(m), rs_loc.at[m])

    def spread(m):
        _, _, _, source, zs, xs, lane = item(m)
        on = (x == lane) & need(m)
        slot = piece_of(m)

        def copy(n, dev):
            return pltpu.make_async_remote_copy(
                src_ref=slot, dst_ref=slot, send_sem=rs_send.at[m, n], recv_sem=rs_sem.at[m],
                device_id=dev, device_id_type=MESH,
            )

        yield (c == source) & (xs != lane) & need(m), copy(0, (r, lax.rem(zs * X + lane, C)))
        yield on & (z >= zs) & (z + 1 < Z), copy(1, (r, lax.rem(c + X, C)))
        yield on & (z <= zs) & (z > 0), copy(2, (r, lax.rem(c + C - X, C)))
        for step in range(1, X):
            other = lax.rem(lane + step, X)
            yield on & jnp.logical_not((z == zs) & (other == xs)), copy(2 + step, (r, z * X + other))

    def start_own(m, carry):
        cond, copy = own_copy(m)
        pl.when(cond)(copy.start)
        return carry

    lax.fori_loop(0, items, start_own, 0)

    def lead_step(n, when):
        i, j = LOWER[n]
        owner = (r == i % R) & (c == j % C)
        slot = part(ld_ref.at[n], r)
        pl.when(owner & when)(ld_local[n])
        wait_recv(jnp.logical_not(owner) & when, slot, ld_sem.at[n])
        return slot

    def lead_swap(n, slot, when):
        for step in range(1, R):
            send(when, slot, slot, ldx_sem.at[n, step - 1], (lax.rem(r + step, R), c))

    def lead_pass(n, early):
        i, j = LOWER[n]
        lane, source = n % X, j % C
        zs, xs = divmod(source, X)
        on = x == lane
        first = on | (c == source)
        when = first if early else jnp.logical_not(first)
        slot = lead_step(n, when)
        if early:
            if lane != xs:
                send(c == source, slot, slot, ld_sem.at[n], (r, zs * X + lane))
            send(on & (z >= zs) & (z + 1 < Z), slot, slot, ld_sem.at[n], (r, lax.rem(c + X, C)))
            send(on & (z <= zs) & (z > 0), slot, slot, ld_sem.at[n], (r, lax.rem(c + C - X, C)))
            for other in range(X):
                if other != lane:
                    cond = on & (z != zs) if other == xs else on
                    send(cond, slot, slot, ld_sem.at[n], (r, z * X + other))
        lead_swap(n, slot, when)

    lead_pass(0, True)
    lead_pass(0, False)
    for early in (True, False):
        for n in range(1, len(LOWER)):
            lead_pass(n, early)

    def own_spread(m, carry):
        cond, copy = own_copy(m)
        pl.when(cond)(copy.wait)
        for go, out in spread(m):
            pl.when(cond & go)(out.start)
        return carry

    lax.fori_loop(0, items, own_spread, 0)

    cs_local = {}
    for k in range(STEPS):
        for b in range(B):
            src, dst = x_ref.at[k // R, b], cs_ref.at[k, b]
            for step in range(1, R):
                send(r == k % R, src, dst, cs_sem.at[k, b], (lax.rem(r + step, R), c))
            cs_local[k, b] = local(r == k % R, src, dst)

    def take(m):
        return pltpu.make_async_remote_copy(
            src_ref=piece_of(m), dst_ref=piece_of(m), send_sem=send_sem.at[0], recv_sem=rs_sem.at[m],
            device_id=(lax.rem(r + 1, R), c), device_id_type=MESH,
        )

    skew = SKEW * jnp.maximum(z - 1, 0)
    deepest = SKEW * max(Z - 2, 0)
    per_slot = -(-items // (STEPS * GROUPS))

    def forward(s):
        m = s - skew

        @pl.when((m >= 0) & (m < items))
        def _():
            _, _, _, source, _, _, lane = item(m)

            @pl.when((x == lane) & (c != source) & need(m))
            def _():
                take(m).wait_recv()
                for go, out in spread(m):
                    pl.when(go)(out.start)

    def slot_work(s):
        for u in range(per_slot):
            forward(s * per_slot + u)

    def lead_tile(n):
        for step in range(1, R):
            q = lax.rem(r + R - step, R)
            wait_recv(r >= 0, part(ld_ref.at[n], q), ldx_sem.at[n, step - 1])
        w_ref[n] = ld_ref[n]

    lead_tile(0)
    for k in range(STEPS):
        invert_factor(w_ref.at[SLOT[k, k]], lambda g, k=k: slot_work(k * GROUPS + g))
        inv = w_ref[SLOT[k, k]]
        if k == 0:
            for n in range(1, len(LOWER)):
                lead_tile(n)
            for i in range(STEPS):

                @pl.when(r == i % R)
                def _():
                    for j in range(STEPS):
                        rs_ref[j, i // R] = ld_ref[SLOT[i, j]] if j <= i else jnp.zeros((T, T), F32)

        for i in range(k + 1, STEPS):
            w_ref[SLOT[i, k]] = dot_nt(w_ref[SLOT[i, k]], inv)
        for j in range(k + 1, STEPS):
            for i in range(j, STEPS):
                w_ref[SLOT[i, j]] = w_ref[SLOT[i, j]] - dot_nt(w_ref[SLOT[i, k]], w_ref[SLOT[j, k]])
    for k in range(STEPS):
        m_ref[SLOT[k, k]] = w_ref[SLOT[k, k]]
        for i in range(k + 1, STEPS):
            total = dot_nn(w_ref[SLOT[i, k]], m_ref[SLOT[k, k]])
            for j in range(k + 1, i):
                total = total + dot_nn(w_ref[SLOT[i, j]], m_ref[SLOT[j, k]])
            m_ref[SLOT[i, k]] = -dot_nn(w_ref[SLOT[i, i]], total)

    def late(s, carry):
        forward(s)
        return carry

    lax.fori_loop(STEPS * GROUPS * per_slot, max(items + deepest, STEPS * GROUPS * per_slot), late, 0)

    def finish_item(m, carry):
        _, _, _, source, _, _, lane = item(m)
        pl.when((x != lane) & (c != source) & need(m))(take(m).wait_recv)
        for go, out in spread(m):
            pl.when(go)(out.wait_send)
        return carry

    lax.fori_loop(0, items, finish_item, 0)
    for k in range(STEPS):
        for b in range(B):
            pl.when(r == k % R)(cs_local[k, b])
            wait_recv(r != k % R, cs_ref.at[k, b], cs_sem.at[k, b])
    for cond, wait in pending:
        pl.when(cond)(wait)


def lead(tiles, R, C):
    A, B, T, _ = tiles.shape
    X, _ = split_col(C)
    n = len(LOWER)
    items = STEPS * A * PIECES
    vmem = pl.BlockSpec(memory_space=pltpu.VMEM)
    sends = n * (R - 1) * 3 + STEPS * B * (R - 1) + n * (X + 2)
    locals_ = n + STEPS * B
    dma = pltpu.SemaphoreType.DMA
    return pl.pallas_call(
        functools.partial(lead_kernel, R, C),
        name="lead",
        out_shape=(
            jax.ShapeDtypeStruct((n, T, T), F32),
            jax.ShapeDtypeStruct((STEPS, A, T, T), F32),
            jax.ShapeDtypeStruct((STEPS, B, T, T), F32),
        ),
        in_specs=[vmem],
        out_specs=(vmem, vmem, vmem),
        scratch_shapes=[
            pltpu.VMEM((n, T, T), F32),
            pltpu.VMEM((n, T, T), F32),
            dma((sends,)), dma((locals_,)), dma((n,)), dma((n, R - 1)), dma((items,)), dma((STEPS, B)),
            dma((items, X + 2)), dma((items,)),
        ],
        compiler_params=pltpu.CompilerParams(has_side_effects=True, vmem_limit_bytes=56 * 2**20),
    )(tiles)


def halves(value):
    high = value.astype(BF16)
    return high, (value - high.astype(F32)).astype(BF16)


def dot3(p, q, dims):
    d = functools.partial(lax.dot_general, dimension_numbers=(dims, ((), ())), preferred_element_type=F32)
    return d(p[0], q[0]) + (d(p[0], q[1]) + d(p[1], q[0]))


NT = ((1,), (1,))
NN = ((1,), (0,))


def finish_kernel(R, C, x_ref, m_ref, rs_ref, cs_ref, t_ref, p_ref, mh_ref, ml_ref, qh_ref, ql_ref):
    A, B, T, _ = x_ref.shape
    r, c = lax.axis_index("row"), lax.axis_index("col")
    for n in range(len(LOWER)):
        mh_ref[n], ml_ref[n] = halves(m_ref[n])
    for b in range(B):
        terms = [halves(cs_ref[j, b]) for j in range(STEPS)]
        for k in range(STEPS):
            total = None
            for j in range(k + 1):
                n = SLOT[k, j]
                term = dot3((mh_ref[n], ml_ref[n]), terms[j], NN)
                total = term if total is None else total + term
            qh_ref[k, b], ql_ref[k, b] = halves(total)

    def body(a, carry):
        tile_row = a * R + r
        terms = [halves(rs_ref[j, a]) for j in range(STEPS)]
        panel = []
        for k in range(STEPS):
            total = None
            for j in range(k + 1):
                n = SLOT[k, j]
                term = dot3(terms[j], (mh_ref[n], ml_ref[n]), NT)
                total = term if total is None else total + term
            p_ref[a, k] = jnp.where(tile_row >= k, total, F32(0.0))
            panel.append(halves(total))
        for b in range(B):
            total = x_ref[a, b]
            for k in range(STEPS):
                total = total - dot3(panel[k], (qh_ref[k, b], ql_ref[k, b]), NN)
            keep = (tile_row >= STEPS) & (b * C + c >= STEPS)
            t_ref[a, :, b * T : (b + 1) * T] = jnp.where(keep, total, F32(0.0))
        return carry

    lax.fori_loop(0, A, body, 0)


def finish(tiles, m, rs, cs, R, C):
    A, B, T, _ = tiles.shape
    vmem = pl.BlockSpec(memory_space=pltpu.VMEM)
    n = len(LOWER)
    return pl.pallas_call(
        functools.partial(finish_kernel, R, C),
        name="finish",
        out_shape=(jax.ShapeDtypeStruct((A, T, B * T), F32), jax.ShapeDtypeStruct((A, STEPS, T, T), F32)),
        in_specs=[vmem] * 4,
        out_specs=(vmem, vmem),
        scratch_shapes=[
            pltpu.VMEM((n, T, T), BF16),
            pltpu.VMEM((n, T, T), BF16),
            pltpu.VMEM((STEPS, B, T, T), BF16),
            pltpu.VMEM((STEPS, B, T, T), BF16),
        ],
        compiler_params=pltpu.CompilerParams(vmem_limit_bytes=56 * 2**20),
    )(tiles, m, rs, cs)


def shards(kernel):
    A, _, T, B, _, _ = kernel.shape
    R, C = lax.axis_size("row"), lax.axis_size("col")
    tiles = kernel.reshape(A, T, B, T).transpose(0, 2, 1, 3)
    m, rs, cs = lead(tiles, R, C)
    trailing, panels = finish(tiles, m, rs, cs, R, C)
    return trailing.reshape(kernel.shape), panels.transpose(0, 2, 1, 3).reshape(A, 1, T, STEPS, T)


def solution(mesh):
    in_specs = (P(None, "row", None, None, "col", None),)
    out_specs = (P(None, "row", None, None, "col", None), P(None, "row", None, None, None))
    return jax.shard_map(shards, mesh=mesh, in_specs=in_specs, out_specs=out_specs, check_vma=False)
```
